32 devices in a mesh: dp: 8 (over y, x, core), mp: 4 (over z).
Axes of the slice: x: 2, y: 2, z: 4, core: 2. Of those that a mesh axis runs over, the one named last changes fastest.
Arguments:
- tokens: bfloat16 [8192, 5120], P('dp'), may hold values from -6 to 6
- norm_gain: bfloat16 [5120], replicated, may hold values from 0.099609375 to 1.8984375
- w_query: bfloat16 [5120, 5120], P('dp', 'mp'), may hold values from -0.078125 to 0.078125
- b_query: bfloat16 [5120], P('mp'), may hold values from -3 to 3
- keyvalue_weight: bfloat16 [5120, 2, 1024], P('dp', None, 'mp'), may hold values from -0.078125 to 0.078125
- b_keyval: bfloat16 [2, 1024], P(None, 'mp'), may hold values from -3 to 3
- w_out: bfloat16 [5120, 5120], P('mp', 'dp'), may hold values from -0.5 to 0.5
- kv_pool: bfloat16 [2, 512, 64, 1024], P(None, 'dp', None, 'mp'), may hold values from -64 to 64
- page_owner: int32 [8, 16], replicated, may hold values from 0 to 7, as said below
- page_index: int32 [8, 16], replicated, may hold values from 0 to 63
- prefix_pages: int32 [8], replicated, may hold values from 10 to 16, as said below
- prompt_device: int32 [8], replicated, may hold values from 0 to 7, each once
Outputs:
- attn_out: bfloat16 [8192, 5120], P('dp', 'mp')
The draws below stay inside these ranges and needn't reach their ends.
Inputs may be any that keep to these rules, and one draw needn't show every extreme that they name: `page_owner`: slots at or beyond a prompt's prefix_pages are unused. Of one prompt's used slots at most 2 name the same owner, and some prompt has exactly 2 used slots with one owner. `prefix_pages`: some prompt has 16 used slots.
All inputs are finite; a program needn't handle non-finite values.
Results may differ from the reference program's by a relative error of at most 0.014.
The reference program's roundings to bfloat16 on the way count: a program that leaves them out, or rounds other values in their place, can miss the bound.
Values may be sent and summed in bfloat16 or wider, within the bound.
A program may use at most 192 MiB of HBM per device.

```python
import jax
import jax.numpy as jnp
from jax import lax

D = 5120
H = 40
KVH = 8
HD = 128
SUFFIX = 1024
PAGE = 64
MAXP = 16
CAP = 2
POOL = 64
TOKENS = 8192
N_DP = 8
N_MP = 4


def page_plan(key):
    base = jax.random.fold_in(key, 7)
    key_len, key_top, key_rating, key_frequent, key_index = jax.random.split(base, 5)
    lengths = jax.random.randint(key_len, (N_DP,), MAXP - 3 * MAXP // 8, MAXP + 1)
    longest = jax.random.randint(key_top, (), 0, N_DP)
    lengths = jnp.where(jnp.arange(N_DP) == longest, MAXP, lengths).astype(jnp.int32)
    frequent_ranking = jax.random.permutation(key_frequent, N_DP)
    frequent_count = max(1, N_DP // 4)
    score_extra = jnp.where(frequent_ranking < frequent_count, 512, 0)
    logit_scores = jax.random.randint(key_rating, (N_DP, N_DP), 0, 1024) - score_extra[None, :]
    distinct = logit_scores * N_DP + jnp.arange(N_DP)[None, :]
    owner_list = jnp.argsort(distinct, axis=1, stable=True)
    slot_run = jnp.broadcast_to((jnp.arange(MAXP) // CAP)[None, :], (N_DP, MAXP))
    owners = jnp.take_along_axis(owner_list, slot_run, axis=1).astype(jnp.int32)
    indices = jax.random.randint(key_index, (N_DP, MAXP), 0, POOL).astype(jnp.int32)
    return (owners, indices, lengths)


def draw_page_owner(key, part):
    return page_plan(key)[0]


def draw_page_index(key, part):
    return page_plan(key)[1]


def draw_prefix_pages(key, part):
    return page_plan(key)[2]


def draw_kv_pool(key, part):
    key_main = jax.random.fold_in(jax.random.fold_in(key, 11), 0)
    shape = (2, N_DP * POOL, PAGE, KVH * HD)
    values = jnp.clip(jax.random.normal(key_main, shape, jnp.float32), -6.0, 6.0)
    return values.astype(jnp.bfloat16)


def block_scale(key, extent, cuts, smallest, top_value):
    def one(position, shards_of):
        heights = jax.random.uniform(jax.random.fold_in(jax.random.fold_in(key, 6), position), (shards_of,), jnp.float32, smallest / len(cuts), top_value / len(cuts))
        return jnp.repeat(jnp.exp(heights), extent[position] // shards_of).reshape((-1,) + (1,) * (len(extent) - position - 1))

    loudness = one(*cuts[0])
    for cut in cuts[1:]:
        loudness = loudness * one(*cut)
    return loudness


def bell_draw(rng, extent, scale, bound, cuts=(), held_as=jnp.bfloat16):
    drawn = scale * jax.random.normal(rng, extent, jnp.float32)
    if cuts:
        drawn = drawn * block_scale(rng, extent, cuts, -0.22, 0.18)
    return jnp.clip(drawn, -bound, bound).astype(held_as)


def setup_inputs(seed: int = 0) -> dict:
    splits = jax.random.split(jax.random.key(seed), 13)
    return {
        "tokens": bell_draw(splits[0], (TOKENS, D), 1.0, 6.0, ((0, 8),)),
        "norm_gain": jnp.clip(1.0 + 0.18 * jax.random.normal(splits[1], (D,), jnp.float32), 0.099609375, 1.8984375).astype(jnp.bfloat16),
        "w_query": bell_draw(splits[2], (D, H * HD), D ** -0.5, 0.078125, ((0, 8), (1, 4))),
        "b_query": bell_draw(splits[3], (H * HD,), 0.5, 3.0, ((0, 4),)),
        "keyvalue_weight": bell_draw(splits[4], (D, 2, KVH * HD), D ** -0.5, 0.078125, ((0, 8), (2, 4))),
        "b_keyval": bell_draw(splits[5], (2, KVH * HD), 0.5, 3.0, ((1, 4),)),
        "w_out": bell_draw(splits[6], (H * HD, D), HD ** -0.5, 0.5, ((0, 4), (1, 8))),
        "kv_pool": draw_kv_pool(jax.random.fold_in(splits[12], 71), 0),
        "page_owner": draw_page_owner(jax.random.fold_in(splits[12], 71), 0),
        "page_index": draw_page_index(jax.random.fold_in(splits[12], 71), 0),
        "prefix_pages": draw_prefix_pages(jax.random.fold_in(splits[12], 71), 0),
        "prompt_device": jax.random.permutation(splits[11], N_DP).astype(jnp.int32),
    }


rope_theta = 1000000.0
norm_eps = 1e-06
masked_score = -1e+30

def rms_normed(rows, norm_gain):
    values = rows.astype(jnp.float32)
    inverse = lax.rsqrt(lax.optimization_barrier(jnp.mean(values * values, axis=-1, keepdims=True)) + norm_eps)
    return (values * inverse * norm_gain.astype(jnp.float32)).astype(jnp.bfloat16)

def rotary(values, positions):
    half_dim = values.shape[-1] // 2
    frequency = rope_theta ** (-jnp.arange(half_dim, dtype=jnp.float32) * 2.0 / values.shape[-1])
    angles = positions.astype(jnp.float32)[:, None] * frequency[None, :]
    cosine = jnp.cos(angles)[:, None, :]
    sine_part = jnp.sin(angles)[:, None, :]
    front_half = values[..., :half_dim]
    back_half = values[..., half_dim:]
    return jnp.concatenate([front_half * cosine - back_half * sine_part, back_half * cosine + front_half * sine_part], axis=-1)

def head_attention(query, keys, values, allowed):
    logit_scores = jnp.einsum('sgd,nd->gsn', query.astype(jnp.float32), keys.astype(jnp.float32)) * HD ** (-0.5)
    logit_scores = jnp.where(allowed[None], logit_scores, masked_score)
    top = lax.optimization_barrier(jnp.max(logit_scores, axis=-1, keepdims=True))
    raised = jnp.exp(logit_scores - top)
    weights = (raised / lax.optimization_barrier(jnp.sum(raised, axis=-1, keepdims=True))).astype(jnp.bfloat16)
    return jnp.einsum('gsn,nd->sgd', weights.astype(jnp.float32), values.astype(jnp.float32)).astype(jnp.bfloat16)

def reference(tokens, norm_gain, w_query, b_query, keyvalue_weight, b_keyval, w_out, kv_pool, page_owner, page_index, prefix_pages, prompt_device):
    slot_prompt = jnp.zeros((N_DP,), jnp.int32).at[prompt_device].set(jnp.arange(N_DP, dtype=jnp.int32))
    token_blocks = tokens.reshape(N_DP, SUFFIX, D)
    flat_keyval = keyvalue_weight.reshape(D, 2 * KVH * HD)

    def one_group(item):
        rows, prompt = item
        normed = rms_normed(rows, norm_gain)
        query = jnp.dot(normed, w_query, preferred_element_type=jnp.float32) + b_query.astype(jnp.float32)
        keyval = jnp.dot(normed, flat_keyval, preferred_element_type=jnp.float32) + b_keyval.reshape(2 * KVH * HD).astype(jnp.float32)
        length = prefix_pages[prompt]
        positions = length * PAGE + jnp.arange(SUFFIX, dtype=jnp.int32)
        rotated = rotary(query.reshape(SUFFIX, H, HD), positions).astype(jnp.bfloat16)
        new_keys = rotary(keyval[:, :KVH * HD].reshape(SUFFIX, KVH, HD), positions).astype(jnp.bfloat16)
        new_values = keyval[:, KVH * HD:].reshape(SUFFIX, KVH, HD).astype(jnp.bfloat16)
        flat_pages = (page_owner[prompt] * POOL + page_index[prompt]).astype(jnp.int32)
        cached = jnp.take(kv_pool, flat_pages, axis=1).reshape(2, MAXP * PAGE, KVH, HD)
        keys = jnp.concatenate([cached[0], new_keys], axis=0)
        values = jnp.concatenate([cached[1], new_values], axis=0)
        page_live = jnp.arange(MAXP * PAGE, dtype=jnp.int32) < length * PAGE
        token_ids = jnp.arange(SUFFIX, dtype=jnp.int32)
        causal = token_ids[None, :] <= token_ids[:, None]
        allowed = jnp.concatenate([jnp.broadcast_to(page_live[None, :], (SUFFIX, MAXP * PAGE)), causal], axis=1)
        grouped = rotated.reshape(SUFFIX, KVH, H // KVH, HD).transpose(1, 0, 2, 3)
        heads_out = lax.map(lambda part: head_attention(part[0], part[1], part[2], allowed), (grouped, keys.transpose(1, 0, 2), values.transpose(1, 0, 2)))
        attended = heads_out.transpose(1, 0, 2, 3).reshape(SUFFIX, H * HD)
        per_shard = attended.reshape(SUFFIX, N_MP, H * HD // N_MP)
        out_rows = w_out.reshape(N_MP, H * HD // N_MP, D)
        total = jnp.zeros((SUFFIX, D), jnp.float32)
        for shard in range(N_MP):
            term = jnp.dot(per_shard[:, shard], out_rows[shard], preferred_element_type=jnp.float32)
            total = total + lax.optimization_barrier(term.astype(jnp.bfloat16)).astype(jnp.float32)
        return total.astype(jnp.bfloat16)
    result = lax.map(one_group, (token_blocks, slot_prompt))
    return result.reshape(N_DP * SUFFIX, D)
```

```python
import functools
import math

import jax
import jax.numpy as jnp
from jax import lax
from jax.experimental import pallas as pl
from jax.experimental.pallas import tpu as pltpu
from jax.sharding import PartitionSpec as P


HD = 128
CAP = 2
ROW_PARTS = 2


rope_theta = 1000000.0
norm_eps = 1e-06
masked_score = -1e30


def rms_normed(rows, norm_gain):
    values = rows.astype(jnp.float32)
    inverse = lax.rsqrt(jnp.mean(values * values, axis=-1, keepdims=True) + norm_eps)
    return (values * inverse * norm_gain.astype(jnp.float32)).astype(jnp.bfloat16)


def rotary_tables(positions):
    half_dim = HD // 2
    frequency = rope_theta ** (-jnp.arange(half_dim, dtype=jnp.float32) * 2.0 / HD)
    angles = positions.astype(jnp.float32)[:, None] * frequency[None, :]
    cosine = jnp.cos(angles)
    sine = jnp.sin(angles)
    return (
        jnp.concatenate([cosine, cosine], axis=-1),
        jnp.concatenate([-sine, sine], axis=-1),
    )


def attention_kernel(block, prev_len, *refs):
    q_ref, k_ref, v_ref, cos_ref, sin_ref, bias_ref, kp_ref, vp_ref = refs[:8]
    refs = refs[8:]
    if prev_len:
        k_prev_ref, v_prev_ref = refs[:2]
        refs = refs[2:]
    o_ref, k_out, v_out = refs
    cosine = cos_ref[...]
    sine = sin_ref[...]

    def rotate(x):
        return (x * cosine + pltpu.roll(x, HD // 2, 1) * sine).astype(jnp.bfloat16)

    @pl.when(pl.program_id(0) == 0)
    def _():
        k_out[...] = rotate(k_ref[...])
        v_out[...] = v_ref[...].astype(jnp.bfloat16)

    query = rotate(q_ref[...])
    factor = HD ** (-0.5) * math.log2(math.e)
    rows = query.shape[0]
    ids = lax.broadcasted_iota(jnp.int32, (block, block), 0)
    keys_id = lax.broadcasted_iota(jnp.int32, (block, block), 1)

    def scores(q, k):
        return lax.dot_general(q, k, (((1,), (1,)), ((), ())), preferred_element_type=jnp.float32)

    for begin in range(0, rows, block):
        q = query[begin : begin + block]
        parts = [(scores(q, kp_ref[0]) + bias_ref[...], vp_ref[0])]
        if prev_len:
            parts.append((scores(q, k_prev_ref[...]), v_prev_ref[...]))
        if begin:
            parts.append((scores(q, k_out[0:begin, :]), v_out[0:begin, :]))
        diagonal = scores(q, k_out[begin : begin + block, :])
        diagonal = jnp.where(keys_id <= ids, diagonal, masked_score)
        parts.append((diagonal, v_out[begin : begin + block, :]))
        top = functools.reduce(
            jnp.maximum, [jnp.max(s, axis=-1, keepdims=True) for s, _ in parts]
        )
        total = None
        out = None
        for s, v in parts:
            raised = jnp.exp2((s - top) * factor)
            row_sum = jnp.sum(raised, axis=-1, keepdims=True)
            term = jnp.dot(raised.astype(jnp.bfloat16), v, preferred_element_type=jnp.float32)
            total = row_sum if total is None else total + row_sum
            out = term if out is None else out + term
        o_ref[begin : begin + block, :] = (out / total).astype(jnp.bfloat16)


def attention(group, qkv, cosine, sine, bias, arrived, prev, per_group):
    rows = qkv.shape[0]
    cached_len = arrived.shape[1]
    block = math.gcd(256, rows)
    const = lambda shape, index: pl.BlockSpec(shape, lambda h: index)
    in_specs = [
        pl.BlockSpec((rows, HD), lambda h: (0, h)),
        const((rows, HD), (0, per_group)),
        const((rows, HD), (0, per_group + 1)),
        const((rows, HD), (0, 0)),
        const((rows, HD), (0, 0)),
        const((1, cached_len), (0, 0)),
        const((1, cached_len, HD), (0, 0, group)),
        const((1, cached_len, HD), (1, 0, group)),
    ]
    operands = [qkv, qkv, qkv, cosine, sine, bias, arrived, arrived]
    prev_len = 0
    if prev is not None:
        prev_len = prev[0].shape[0]
        in_specs += [const((prev_len, HD), (0, 0))] * 2
        operands += list(prev)
    keys = cached_len + prev_len + rows
    return pl.pallas_call(
        functools.partial(attention_kernel, block, prev_len),
        grid=(per_group,),
        in_specs=in_specs,
        out_specs=[
            pl.BlockSpec((rows, HD), lambda h: (0, h)),
            const((rows, HD), (0, 0)),
            const((rows, HD), (0, 0)),
        ],
        out_shape=[
            jax.ShapeDtypeStruct((rows, per_group * HD), jnp.bfloat16),
            jax.ShapeDtypeStruct((rows, HD), jnp.bfloat16),
            jax.ShapeDtypeStruct((rows, HD), jnp.bfloat16),
        ],
        compiler_params=pltpu.CompilerParams(
            dimension_semantics=("arbitrary",), vmem_limit_bytes=40 * 1024 * 1024
        ),
        cost_estimate=pl.CostEstimate(
            flops=8 * per_group * rows * keys * HD,
            bytes_accessed=6 * rows * (per_group + 2) * HD,
            transcendentals=per_group * rows * keys,
        ),
    )(*operands)


def exchange(x, axis, split_axis, concat_axis):
    size = lax.axis_size(axis)
    me = lax.axis_index(axis)
    width = x.shape[split_axis] // size
    span = x.shape[concat_axis]
    shape = list(x.shape)
    shape[split_axis] = width
    shape[concat_axis] = span * size
    result = jnp.zeros(shape, x.dtype)
    for s in range(size):
        target = lax.rem(me + s, size)
        source = lax.rem(me - s + size, size)
        piece = lax.dynamic_slice_in_dim(x, target * width, width, split_axis)
        if s:
            piece = lax.ppermute(piece, axis, [(i, (i + s) % size) for i in range(size)])
        result = lax.dynamic_update_slice_in_dim(result, piece, source * span, concat_axis)
    return result


def layer(
    tokens,
    norm_gain,
    w_query,
    b_query,
    keyvalue_weight,
    b_keyval,
    w_out,
    kv_pool,
    page_owner,
    page_index,
    prefix_pages,
    prompt_device,
):
    groups = lax.axis_size("dp")
    planes = lax.axis_size("mp")
    my_group = lax.axis_index("dp")
    my_plane = lax.axis_index("mp")
    seq_rows = tokens.shape[0]
    width_kv = keyvalue_weight.shape[2]
    kv_local = width_kv // HD
    heads_local = w_query.shape[1] // HD
    per_group = heads_local // kv_local
    page_len = kv_pool.shape[2]
    max_pages = page_owner.shape[1]
    group_ids = jnp.arange(groups, dtype=jnp.int32)

    width_q = per_group * HD
    gathered = []
    biases = []
    for g in range(kv_local):
        piece = jnp.concatenate(
            [
                w_query[:, g * width_q : (g + 1) * width_q],
                keyvalue_weight[:, 0, g * HD : (g + 1) * HD],
                keyvalue_weight[:, 1, g * HD : (g + 1) * HD],
            ],
            axis=1,
        )
        gathered.append(lax.all_gather(piece, "dp", axis=0, tiled=True))
        biases.append(
            jnp.concatenate(
                [
                    b_query[g * width_q : (g + 1) * width_q],
                    b_keyval[0, g * HD : (g + 1) * HD],
                    b_keyval[1, g * HD : (g + 1) * HD],
                ]
            ).astype(jnp.float32)
        )

    slot_prompt = jnp.sum(
        jnp.where(prompt_device[None, :] == group_ids[:, None], group_ids[None, :], 0), axis=1
    )
    owners_all = jnp.take(page_owner, slot_prompt, axis=0)
    index_all = jnp.take(page_index, slot_prompt, axis=0)
    length_all = jnp.take(prefix_pages, slot_prompt, axis=0)
    slot_ids = jnp.arange(max_pages, dtype=jnp.int32)
    places = jnp.arange(CAP, dtype=jnp.int32)
    used = slot_ids[None, :] < length_all[:, None]
    mine = used & (owners_all == my_group)
    rank = jnp.cumsum(mine.astype(jnp.int32), axis=1) - 1
    chosen = mine[:, None, :] & (rank[:, None, :] == places[None, :, None])
    send_index = jnp.sum(jnp.where(chosen, index_all[:, None, :], 0), axis=2)
    outgoing = jnp.take(kv_pool, send_index.reshape(-1), axis=1).reshape(
        2, groups, CAP, page_len, width_kv
    )
    arrived = lax.all_to_all(outgoing, "dp", split_axis=1, concat_axis=1, tiled=True)
    my_owners = jnp.take(owners_all, my_group, axis=0)
    my_length = jnp.take(length_all, my_group, axis=0)
    my_used = slot_ids < my_length
    counts = jnp.sum(
        ((my_owners[None, :] == group_ids[:, None]) & my_used[None, :]).astype(jnp.int32), axis=1
    )
    page_live = (places[None, :] < counts[:, None]).reshape(-1)
    cached_len = page_live.shape[0] * page_len
    arrived = arrived.reshape(2, cached_len, width_kv)
    bias = jnp.where(jnp.repeat(page_live, page_len), 0.0, masked_score).astype(jnp.float32)[None]

    normed = rms_normed(tokens, norm_gain)
    arrived, w_out = lax.optimization_barrier((arrived, w_out))
    out_rows = exchange(w_out, "dp", 0, 1)
    out_rows = exchange(out_rows, "mp", 1, 0)
    out_weight = lax.all_gather(out_rows, "dp", axis=0, tiled=True)
    out_cols = out_weight.shape[1]
    out_weight = out_weight.reshape(groups, planes, -1, out_cols)
    cosine, sine = rotary_tables(
        my_length * page_len + jnp.arange(seq_rows, dtype=jnp.int32)
    )
    part = seq_rows // ROW_PARTS
    held = [[[] for _ in range(ROW_PARTS)] for _ in range(planes)]
    for g in range(kv_local):
        prev = None
        for r in range(ROW_PARTS):
            rows = slice(r * part, (r + 1) * part)
            qkv = (
                jnp.dot(normed[rows], gathered[g], preferred_element_type=jnp.float32)
                + biases[g]
            )
            attended, keys, values = attention(
                g, qkv, cosine[rows], sine[rows], bias, arrived, prev, per_group
            )
            if prev is None:
                prev = (keys, values)
            else:
                prev = (
                    jnp.concatenate([prev[0], keys], axis=0),
                    jnp.concatenate([prev[1], values], axis=0),
                )
            held[0][r].append(attended)
            for s in range(1, planes):
                held[s][r].append(
                    lax.ppermute(
                        attended, "mp", [(i, (i + s) % planes) for i in range(planes)]
                    )
                )
    weights = []
    for s in range(planes):
        source = lax.rem(my_plane - s + planes, planes)
        rows_of = lax.dynamic_index_in_dim(out_weight, source, axis=1, keepdims=False)
        weights.append(rows_of.reshape(-1, out_cols))
    outputs = []
    for r in range(ROW_PARTS):
        total = None
        for s in range(planes):
            head_partial = None
            for g in range(kv_local):
                term = jnp.dot(
                    held[s][r][g],
                    weights[s][g * width_q : (g + 1) * width_q],
                    preferred_element_type=jnp.float32,
                )
                head_partial = term if head_partial is None else term + head_partial
            head_partial = head_partial.astype(jnp.bfloat16).astype(jnp.float32)
            total = head_partial if total is None else total + head_partial
        outputs.append(total.astype(jnp.bfloat16))
    return jnp.concatenate(outputs, axis=0)


def solution(mesh):
    return jax.shard_map(
        layer,
        mesh=mesh,
        in_specs=(
            P("dp", None),
            P(),
            P("dp", "mp"),
            P("mp"),
            P("dp", None, "mp"),
            P(None, "mp"),
            P("mp", "dp"),
            P(None, "dp", None, "mp"),
            P(),
            P(),
            P(),
            P(),
        ),
        out_specs=P("dp", "mp"),
        check_vma=False,
    )
```

```python
import functools
import math

import jax
import jax.numpy as jnp
from jax import lax
from jax.experimental import pallas as pl
from jax.experimental.pallas import tpu as pltpu
from jax.sharding import PartitionSpec as P


HD = 128
CAP = 2
ROW_PARTS = 2


rope_theta = 1000000.0
norm_eps = 1e-06
masked_score = -1e30


def rms_normed(rows, norm_gain):
    values = rows.astype(jnp.float32)
    inverse = lax.rsqrt(jnp.mean(values * values, axis=-1, keepdims=True) + norm_eps)
    return (values * inverse * norm_gain.astype(jnp.float32)).astype(jnp.bfloat16)


def rotary_tables(positions):
    half_dim = HD // 2
    frequency = rope_theta ** (-jnp.arange(half_dim, dtype=jnp.float32) * 2.0 / HD)
    angles = positions.astype(jnp.float32)[:, None] * frequency[None, :]
    cosine = jnp.cos(angles)
    sine = jnp.sin(angles)
    return (
        jnp.concatenate([cosine, cosine], axis=-1),
        jnp.concatenate([-sine, sine], axis=-1),
    )


def attention_kernel(block, prev_len, *refs):
    q_ref, k_ref, v_ref, cos_ref, sin_ref, bias_ref, kp_ref, vp_ref = refs[:8]
    refs = refs[8:]
    if prev_len:
        k_prev_ref, v_prev_ref = refs[:2]
        refs = refs[2:]
    o_ref, k_out, v_out = refs
    cosine = cos_ref[...]
    sine = sin_ref[...]

    def rotate(x):
        return (x * cosine + pltpu.roll(x, HD // 2, 1) * sine).astype(jnp.bfloat16)

    @pl.when(pl.program_id(0) == 0)
    def _():
        k_out[...] = rotate(k_ref[...])
        v_out[...] = v_ref[...].astype(jnp.bfloat16)

    query = rotate(q_ref[...])
    factor = HD ** (-0.5) * math.log2(math.e)
    rows = query.shape[0]
    ids = lax.broadcasted_iota(jnp.int32, (block, block), 0)
    keys_id = lax.broadcasted_iota(jnp.int32, (block, block), 1)

    def scores(q, k):
        return lax.dot_general(q, k, (((1,), (1,)), ((), ())), preferred_element_type=jnp.float32)

    for begin in range(0, rows, block):
        q = query[begin : begin + block]
        parts = [(scores(q, kp_ref[0]) + bias_ref[...], vp_ref[0])]
        if prev_len:
            parts.append((scores(q, k_prev_ref[...]), v_prev_ref[...]))
        if begin:
            parts.append((scores(q, k_out[0:begin, :]), v_out[0:begin, :]))
        diagonal = scores(q, k_out[begin : begin + block, :])
        diagonal = jnp.where(keys_id <= ids, diagonal, masked_score)
        parts.append((diagonal, v_out[begin : begin + block, :]))
        top = functools.reduce(
            jnp.maximum, [jnp.max(s, axis=-1, keepdims=True) for s, _ in parts]
        )
        total = None
        out = None
        for s, v in parts:
            raised = jnp.exp2((s - top) * factor)
            row_sum = jnp.sum(raised, axis=-1, keepdims=True)
            term = jnp.dot(raised.astype(jnp.bfloat16), v, preferred_element_type=jnp.float32)
            total = row_sum if total is None else total + row_sum
            out = term if out is None else out + term
        o_ref[begin : begin + block, :] = (out / total).astype(jnp.bfloat16)


def attention(group, qkv, cosine, sine, bias, arrived, prev, per_group):
    rows = qkv.shape[0]
    cached_len = arrived.shape[1]
    block = math.gcd(256, rows)
    const = lambda shape, index: pl.BlockSpec(shape, lambda h: index)
    in_specs = [
        pl.BlockSpec((rows, HD), lambda h: (0, h)),
        const((rows, HD), (0, per_group)),
        const((rows, HD), (0, per_group + 1)),
        const((rows, HD), (0, 0)),
        const((rows, HD), (0, 0)),
        const((1, cached_len), (0, 0)),
        const((1, cached_len, HD), (0, 0, group)),
        const((1, cached_len, HD), (1, 0, group)),
    ]
    operands = [qkv, qkv, qkv, cosine, sine, bias, arrived, arrived]
    prev_len = 0
    if prev is not None:
        prev_len = prev[0].shape[0]
        in_specs += [const((prev_len, HD), (0, 0))] * 2
        operands += list(prev)
    keys = cached_len + prev_len + rows
    return pl.pallas_call(
        functools.partial(attention_kernel, block, prev_len),
        grid=(per_group,),
        in_specs=in_specs,
        out_specs=[
            pl.BlockSpec((rows, HD), lambda h: (0, h)),
            const((rows, HD), (0, 0)),
            const((rows, HD), (0, 0)),
        ],
        out_shape=[
            jax.ShapeDtypeStruct((rows, per_group * HD), jnp.bfloat16),
            jax.ShapeDtypeStruct((rows, HD), jnp.bfloat16),
            jax.ShapeDtypeStruct((rows, HD), jnp.bfloat16),
        ],
        compiler_params=pltpu.CompilerParams(
            dimension_semantics=("arbitrary",), vmem_limit_bytes=40 * 1024 * 1024
        ),
        cost_estimate=pl.CostEstimate(
            flops=8 * per_group * rows * keys * HD,
            bytes_accessed=6 * rows * (per_group + 2) * HD,
            transcendentals=per_group * rows * keys,
        ),
    )(*operands)


def exchange(x, axis, split_axis, concat_axis):
    size = lax.axis_size(axis)
    me = lax.axis_index(axis)
    width = x.shape[split_axis] // size
    span = x.shape[concat_axis]
    shape = list(x.shape)
    shape[split_axis] = width
    shape[concat_axis] = span * size
    result = jnp.zeros(shape, x.dtype)
    for s in range(size):
        target = lax.rem(me + s, size)
        source = lax.rem(me - s + size, size)
        piece = lax.dynamic_slice_in_dim(x, target * width, width, split_axis)
        if s:
            piece = lax.ppermute(piece, axis, [(i, (i + s) % size) for i in range(size)])
        result = lax.dynamic_update_slice_in_dim(result, piece, source * span, concat_axis)
    return result


def layer(
    tokens,
    norm_gain,
    w_query,
    b_query,
    keyvalue_weight,
    b_keyval,
    w_out,
    kv_pool,
    page_owner,
    page_index,
    prefix_pages,
    prompt_device,
):
    groups = lax.axis_size("dp")
    planes = lax.axis_size("mp")
    my_group = lax.axis_index("dp")
    my_plane = lax.axis_index("mp")
    seq_rows = tokens.shape[0]
    width_kv = keyvalue_weight.shape[2]
    kv_local = width_kv // HD
    heads_local = w_query.shape[1] // HD
    per_group = heads_local // kv_local
    page_len = kv_pool.shape[2]
    max_pages = page_owner.shape[1]
    group_ids = jnp.arange(groups, dtype=jnp.int32)

    width_q = per_group * HD
    gathered = []
    biases = []
    for g in range(kv_local):
        piece = jnp.concatenate(
            [
                w_query[:, g * width_q : (g + 1) * width_q],
                keyvalue_weight[:, 0, g * HD : (g + 1) * HD],
                keyvalue_weight[:, 1, g * HD : (g + 1) * HD],
            ],
            axis=1,
        )
        gathered.append(lax.all_gather(piece, "dp", axis=0, tiled=True))
        biases.append(
            jnp.concatenate(
                [
                    b_query[g * width_q : (g + 1) * width_q],
                    b_keyval[0, g * HD : (g + 1) * HD],
                    b_keyval[1, g * HD : (g + 1) * HD],
                ]
            ).astype(jnp.float32)
        )

    slot_prompt = jnp.sum(
        jnp.where(prompt_device[None, :] == group_ids[:, None], group_ids[None, :], 0), axis=1
    )
    owners_all = jnp.take(page_owner, slot_prompt, axis=0)
    index_all = jnp.take(page_index, slot_prompt, axis=0)
    length_all = jnp.take(prefix_pages, slot_prompt, axis=0)
    slot_ids = jnp.arange(max_pages, dtype=jnp.int32)
    places = jnp.arange(CAP, dtype=jnp.int32)
    used = slot_ids[None, :] < length_all[:, None]
    mine = used & (owners_all == my_group)
    rank = jnp.cumsum(mine.astype(jnp.int32), axis=1) - 1
    chosen = mine[:, None, :] & (rank[:, None, :] == places[None, :, None])
    send_index = jnp.sum(jnp.where(chosen, index_all[:, None, :], 0), axis=2)
    outgoing = jnp.take(kv_pool, send_index.reshape(-1), axis=1).reshape(
        2, groups, CAP, page_len, width_kv
    )
    arrived = lax.all_to_all(outgoing, "dp", split_axis=1, concat_axis=1, tiled=True)
    my_owners = jnp.take(owners_all, my_group, axis=0)
    my_length = jnp.take(length_all, my_group, axis=0)
    my_used = slot_ids < my_length
    counts = jnp.sum(
        ((my_owners[None, :] == group_ids[:, None]) & my_used[None, :]).astype(jnp.int32), axis=1
    )
    page_live = (places[None, :] < counts[:, None]).reshape(-1)
    cached_len = page_live.shape[0] * page_len
    arrived = arrived.reshape(2, cached_len, width_kv)
    bias = jnp.where(jnp.repeat(page_live, page_len), 0.0, masked_score).astype(jnp.float32)[None]

    normed = rms_normed(tokens, norm_gain)
    arrived, w_out = lax.optimization_barrier((arrived, w_out))
    out_rows = exchange(w_out, "dp", 0, 1)
    out_rows = exchange(out_rows, "mp", 1, 0)
    out_weight = lax.all_gather(out_rows, "dp", axis=0, tiled=True)
    out_cols = out_weight.shape[1]
    out_weight = out_weight.reshape(groups, planes, -1, out_cols)
    cosine, sine = rotary_tables(
        my_length * page_len + jnp.arange(seq_rows, dtype=jnp.int32)
    )
    part = seq_rows // ROW_PARTS
    held = [[[] for _ in range(ROW_PARTS)] for _ in range(planes)]
    for g in range(kv_local):
        prev = None
        for r in range(ROW_PARTS):
            rows = slice(r * part, (r + 1) * part)
            qkv = (
                jnp.dot(normed[rows], gathered[g], preferred_element_type=jnp.float32)
                + biases[g]
            )
            attended, keys, values = attention(
                g, qkv, cosine[rows], sine[rows], bias, arrived, prev, per_group
            )
            if prev is None:
                prev = (keys, values)
            else:
                prev = (
                    jnp.concatenate([prev[0], keys], axis=0),
                    jnp.concatenate([prev[1], values], axis=0),
                )
            held[0][r].append(attended)
            for s in range(1, planes):
                high = 1 << (s.bit_length() - 1)
                low = s - high
                _, moved, step = ("relay", held[high][r][g], low) if low else ("send", attended, s)
                held[s][r].append(lax.ppermute(moved, "mp", [(i, i ^ step) for i in range(planes)]))
    weights = []
    for s in range(planes):
        source = my_plane ^ s
        rows_of = lax.dynamic_index_in_dim(out_weight, source, axis=1, keepdims=False)
        weights.append(rows_of.reshape(-1, out_cols))
    outputs = []
    for r in range(ROW_PARTS):
        total = None
        for s in range(planes):
            head_partial = None
            for g in range(kv_local):
                term = jnp.dot(
                    held[s][r][g],
                    weights[s][g * width_q : (g + 1) * width_q],
                    preferred_element_type=jnp.float32,
                )
                head_partial = term if head_partial is None else term + head_partial
            head_partial = head_partial.astype(jnp.bfloat16).astype(jnp.float32)
            total = head_partial if total is None else total + head_partial
        outputs.append(total.astype(jnp.bfloat16))
    return jnp.concatenate(outputs, axis=0)


def solution(mesh):
    return jax.shard_map(
        layer,
        mesh=mesh,
        in_specs=(
            P("dp", None),
            P(),
            P("dp", "mp"),
            P("mp"),
            P("dp", None, "mp"),
            P(None, "mp"),
            P("mp", "dp"),
            P(None, "dp", None, "mp"),
            P(),
            P(),
            P(),
            P(),
        ),
        out_specs=P("dp", "mp"),
        check_vma=False,
    )
```
